32 devices in a mesh: dp: 4 (over y, core), expert: 8 (over z, x).
Axes of the slice: x: 2, y: 2, z: 4, core: 2. Of those that a mesh axis runs over, the one named last changes fastest.
Arguments:
- tokens: bfloat16 [32768, 768], P(('dp', 'expert')), may hold values from -6 to 6
- lengths: int32 [32], P(('dp', 'expert')), may hold values from 144 to 1024, as said below
- routes: int32 [32768], P(('dp', 'expert')), may hold values from 0 to 7, as said below
- attn_in: bfloat16 [2304, 768], P(('dp', 'expert')), may hold values from -0.21875 to 0.21875
- attn_out: bfloat16 [768, 768], P(('dp', 'expert')), may hold values from -3.5 to 3.5
- ln_gain: bfloat16 [2, 768], P(None, ('dp', 'expert')), may hold values from 0.25 to 1.75
- ln_bias: bfloat16 [2, 768], P(None, ('dp', 'expert')), may hold values from -1.1953125 to 1.1953125
- w_in: bfloat16 [8, 768, 3072], P('expert', None, 'dp'), may hold values from -0.21875 to 0.21875
- w_out: bfloat16 [8, 3072, 768], P('expert', 'dp'), may hold values from -0.109375 to 0.109375
- cotangent: bfloat16 [32768, 768], P(('dp', 'expert')), may hold values from -6 to 6
Outputs:
- block_out: bfloat16 [32768, 768], P(('dp', 'expert'))
- grad_tokens: float32 [32768, 768], P(('dp', 'expert'))
- grad_attn_in: float32 [2304, 768], P(('dp', 'expert'))
- grad_attn_out: float32 [768, 768], P(('dp', 'expert'))
- grad_gain: float32 [2, 768], P(None, ('dp', 'expert'))
- grad_bias: float32 [768], P(('dp', 'expert'))
- grad_bias_moe: float32 [768], P(('dp', 'expert'))
- grad_w_in: float32 [8, 768, 3072], P('expert', None, 'dp')
- grad_w_out: float32 [8, 3072, 768], P('expert', 'dp')
The draws below stay inside these ranges and needn't reach their ends.
Inputs may be any that keep to these rules, and one draw needn't show every extreme that they name: `lengths`: every draw has a sequence of the full 1024 positions. `routes`: among the valid tokens of one sequence, at most 144 name the same expert; in every draw some expert receives exactly 144 valid tokens from every sequence of some index of dp.
All inputs are finite; a program needn't handle non-finite values.
Results may differ from the reference program's by a relative error of at most 0.012.
Values may be sent and summed in bfloat16 or wider, within the bound.
No kernel may reach another device: no remote copies, remote signals or barrier semaphores. Data moves between devices by JAX's collectives and lax.ppermute only.
A program may use at most 256 MiB of HBM per device.

```python
from functools import partial
import jax
import jax.numpy as jnp
from jax import lax

D = 768
FF = 3072
HEADS = 12
HEAD_DIM = 64
TOK_DEV = 1024
EXPERTS = 8
CAP = 144
LEN_MIN = 144
SEQS = 32
TOKENS = 32768


def draw_lengths(key, part):
    first_key, second_key = jax.random.split(key)
    drawn = jax.random.randint(first_key, (SEQS,), LEN_MIN, TOK_DEV + 1)
    chosen = jax.random.randint(second_key, (), 0, SEQS)
    return jnp.where(jnp.arange(SEQS) == chosen, TOK_DEV, drawn).astype(jnp.int32)


def route_block(block_key, busiest):
    count_key, order_key, pick_key = jax.random.split(block_key, 3)
    least_count = min(CAP, (TOK_DEV - CAP + EXPERTS - 2) // (EXPERTS - 1))
    counts = jax.random.randint(count_key, (EXPERTS,), least_count, CAP + 1)
    counts = jnp.where(jnp.arange(EXPERTS) == busiest, 0, counts)
    entries = jnp.arange(EXPERTS * CAP)
    labels = entries // CAP
    usable = (entries % CAP < counts[labels]).astype(jnp.int32)
    shuffle = jax.random.permutation(order_key, EXPERTS * CAP)
    labels = labels[shuffle]
    usable = usable[shuffle]
    ranking = jnp.argsort(1 - usable, stable=True)
    pool_labels = labels[ranking][:TOK_DEV - CAP]
    picked = jax.random.permutation(pick_key, LEN_MIN)[:CAP]
    chosen = jnp.zeros((TOK_DEV,), jnp.int32).at[picked].set(1)
    others = jnp.cumsum(1 - chosen) - 1
    filled = pool_labels[jnp.clip(others, 0, TOK_DEV - CAP - 1)]
    return jnp.where(chosen == 1, busiest, filled)


def group_expert(key, group):
    return jax.random.randint(jax.random.fold_in(key, 7919 + group), (), 0, EXPERTS)


def draw_routes(key, part):
    blocks = jnp.arange(SEQS)
    busiest = jax.vmap(partial(group_expert, key))(blocks // EXPERTS)
    block_keys = jax.vmap(partial(jax.random.fold_in, key))(blocks)
    return jax.vmap(route_block)(block_keys, busiest).reshape(-1).astype(jnp.int32)


def raised(array, stream_key, source, target, parts, factor):
    owner, partner = [(jnp.arange(array.shape[axis_at]) // (array.shape[axis_at] // parts)).reshape([-1 if axis == axis_at else 1 for axis in range(array.ndim)]) for axis_at in (source, target)]
    chosen = jax.random.permutation(stream_key, parts)[partner]
    strong = (owner == chosen) | (owner == (partner + parts // 2) % parts)
    return jnp.where(strong, factor * array, array)


def block_scale(stream_key, extent, cuts, least, high):
    level = 1.0
    for dim, parts in cuts:
        steps = jax.random.uniform(jax.random.fold_in(jax.random.fold_in(stream_key, 6), dim), (parts,), jnp.float32, least / len(cuts), high / len(cuts))
        level = level * jnp.repeat(jnp.exp(steps), extent[dim] // parts).reshape((-1,) + (1,) * (len(extent) - 1 - dim))
    return level


def normal_values(key, extent, scale, bound, cuts=(), kind=jnp.bfloat16):
    values = jax.random.normal(key, extent, jnp.float32) * scale
    if len(cuts) > 0:
        values = block_scale(key, extent, cuts, -0.22, 0.18) * values
    return jnp.clip(values, min=-bound, max=bound).astype(kind)


def gaussian_with(stream_key, dims, scale, limit, cuts, heavy, kind=jnp.bfloat16):
    values = scale * jax.random.normal(stream_key, dims, jnp.float32)
    if cuts:
        values = values * block_scale(stream_key, dims, cuts, -0.22, 0.18)
    return jnp.clip(raised(values, jax.random.fold_in(stream_key, 3), *heavy), -limit, limit).astype(kind)


def setup_inputs(seed: int = 0) -> dict:
    keys = jax.random.split(jax.random.key(seed), 11)
    tokens = gaussian_with(keys[0], (TOKENS, D), 1.0, 6.0, ((0, 32),), (0, 1, 32, 2.75))
    lengths = draw_lengths(jax.random.fold_in(keys[10], 71), 0)
    routes = draw_routes(jax.random.fold_in(keys[10], 71), 0)
    attn_in = normal_values(keys[3], (3 * D, D), D ** -0.5, 0.21875, ((0, 32),))
    attn_out = normal_values(keys[4], (D, D), (max(1, D // 256)) ** -0.5, 3.5, ((0, 32),))
    ln_gain = jnp.clip(1.0 + 0.15 * jax.random.normal(keys[5], (2, D), jnp.float32), 0.25, 1.75).astype(jnp.bfloat16)
    ln_bias = normal_values(keys[6], (2, D), 0.3, 1.1953125, ((1, 32),))
    w_in = normal_values(keys[7], (EXPERTS, D, FF), D ** -0.5, 0.21875, ((0, 8), (2, 4)))
    w_out = normal_values(keys[8], (EXPERTS, FF, D), FF ** -0.5, 0.109375, ((0, 8), (1, 4)))
    cotangent = normal_values(keys[9], (TOKENS, D), 1.0, 6.0, ((0, 32),))
    return {"tokens": tokens, "lengths": lengths, "routes": routes, "attn_in": attn_in, "attn_out": attn_out, "ln_gain": ln_gain, "ln_bias": ln_bias, "w_in": w_in, "w_out": w_out, "cotangent": cotangent}


@jax.custom_vjp
def low(v):
    return lax.optimization_barrier(v.astype(jnp.bfloat16)).astype(jnp.float32)

@jax.custom_vjp
def low_back(v):
    return v

def low_keep(v):
    return (low(v), None)

def low_pass(kept, grad):
    return (grad,)

def back_keep(v):
    return (v, None)

def back_low(kept, grad):
    return (low(grad),)
low.defvjp(low_keep, low_pass)
low_back.defvjp(back_keep, back_low)
eps = 1e-05
masked_score = -1e+30

def product(left, right):
    return jnp.dot(left, right, precision=lax.Precision.HIGHEST)

def layer_norm(values, gain, shift):
    centre = lax.optimization_barrier(jnp.mean(values, axis=-1, keepdims=True))
    centred = values - centre
    spread = lax.optimization_barrier(jnp.mean(centred * centred, axis=-1, keepdims=True))
    return centred * lax.rsqrt(spread + eps) * gain + shift

def attend(pieces):
    query, key_rows, value_rows, length = pieces
    seq_len = query.shape[0]
    position = jnp.arange(seq_len, dtype=jnp.int32)
    allowed = (position[None, :] <= position[:, None]) & (position[None, :] < length)
    scores = jnp.einsum('qhd,khd->hqk', query, key_rows, precision=lax.Precision.HIGHEST) * HEAD_DIM ** (-0.5)
    scores = low_back(scores)
    scores = jnp.where(allowed[None], scores, masked_score)
    top_score = lax.optimization_barrier(jnp.max(scores, axis=-1, keepdims=True))
    weights = jnp.exp(scores - top_score)
    probs = low(weights / lax.optimization_barrier(jnp.sum(weights, axis=-1, keepdims=True)))
    return jnp.einsum('hqk,khd->qhd', probs, value_rows, precision=lax.Precision.HIGHEST)

def reference(tokens, lengths, routes, attn_in, attn_out, ln_gain, ln_bias, w_in, w_out, cotangent):
    total_rows, model_width = tokens.shape
    seq_count = lengths.shape[0]
    seq_len = total_rows // seq_count
    expert_count = w_in.shape[0]
    position = jnp.arange(total_rows, dtype=jnp.int32) % seq_len
    valid = position < jnp.repeat(lengths, seq_len)
    onehot = ((routes[:, None] == jnp.arange(expert_count, dtype=jnp.int32)[None, :]) & valid[:, None]).astype(jnp.int32)
    ranks = lax.optimization_barrier(jnp.sum((jnp.cumsum(onehot, axis=0) - 1) * onehot, axis=1))
    slot_count = seq_count * CAP
    target = jnp.where(valid, routes * slot_count + ranks, expert_count * slot_count).astype(jnp.int32)
    table = jnp.full((expert_count * slot_count,), total_rows, jnp.int32)
    table = table.at[target].set(jnp.arange(total_rows, dtype=jnp.int32), mode='drop')
    table = table.reshape(expert_count, slot_count)

    def forward(tokens_f, attn_in_f, attn_out_f, gain_f, bias_f, w_in_f, w_out_f):
        normed = low(layer_norm(tokens_f, gain_f[0], bias_f[0]))
        shaped = (seq_count, seq_len, HEADS, HEAD_DIM)
        query = low_back(low(product(normed, attn_in_f[:model_width]))).reshape(shaped)
        key_rows = low_back(low(product(normed, attn_in_f[model_width:2 * model_width]))).reshape(shaped)
        value_rows = low_back(low(product(normed, attn_in_f[2 * model_width:]))).reshape(shaped)
        mixed = lax.map(jax.checkpoint(attend), (query, key_rows, value_rows, lengths))
        mixed = low_back(low(mixed.reshape(total_rows, model_width)))
        hidden = tokens_f + low_back(product(mixed, attn_out_f))
        moe_in = low_back(low(layer_norm(hidden, gain_f[1], bias_f[1])))

        def expert_apply(pieces):
            weight_in, weight_out, row_index = pieces
            picked = jnp.take(moe_in, row_index, axis=0, mode='fill', fill_value=0.0)
            pre = low_back(product(picked, weight_in))
            act = low(jax.nn.gelu(pre, approximate=False))
            return low_back(low(product(act, weight_out)))
        results = lax.map(jax.checkpoint(expert_apply), (w_in_f, w_out_f, table))
        expert_term = jnp.zeros_like(hidden).at[table.reshape(-1)].add(results.reshape(-1, model_width), mode='drop')
        return hidden + expert_term
    arrays = [item.astype(jnp.float32) for item in (tokens, attn_in, attn_out, ln_gain, ln_bias, w_in, w_out)]
    result, pull = jax.vjp(forward, *arrays)
    grads = pull(cotangent.astype(jnp.float32))
    return (result.astype(jnp.bfloat16), grads[0], grads[1], grads[2], grads[3], grads[4][0], grads[4][1], grads[5], grads[6])
```

```python
import math
import jax
import jax.numpy as jnp
from jax import lax
from jax.experimental import pallas as pl
from jax.experimental.pallas import tpu as pltpu
from jax.sharding import Mesh
from jax.sharding import PartitionSpec as P

HEADS = 12
HEAD_DIM = 64
eps = 1e-05
masked_score = -1e30
bf = jnp.bfloat16
f32 = jnp.float32
VMEM_LIMIT = 60 << 20
EVERY = ("y", "core", "z", "x")
RING = ("y", "z", "x")
EXPERT = ("z", "x")


def dot_nt(left, right):
    return lax.dot_general(left, right, (((1,), (1,)), ((), ())), preferred_element_type=f32)


def dot_nn(left, right):
    return lax.dot_general(left, right, (((1,), (0,)), ((), ())), preferred_element_type=f32)


def dot_tn(left, right):
    return lax.dot_general(left, right, (((0,), (0,)), ((), ())), preferred_element_type=f32)


def params(**kw):
    return pltpu.CompilerParams(vmem_limit_bytes=VMEM_LIMIT, **kw)


def split3(x):
    high = x.astype(bf)
    rest = x - high.astype(f32)
    mid = rest.astype(bf)
    return high, mid, (rest - mid.astype(f32)).astype(bf)


def lane_iota(shape):
    return lax.broadcasted_iota(jnp.int32, shape, len(shape) - 1)


def attn_fwd_kernel(tile, len_ref, q_ref, k_ref, v_ref, mixed_ref, qa_ref, ka_ref):
    n = q_ref.shape[0]
    lane = lane_iota((n, 128))
    key_pos = lax.broadcasted_iota(jnp.int32, (n, 128), 0)
    bias = jnp.where(key_pos < len_ref[0], 0.0, masked_score).astype(bf)
    q = q_ref[...] * bf(HEAD_DIM**-0.5)
    k = k_ref[...]
    v = v_ref[...]
    zero = jnp.zeros((n, 128), bf)
    one = jnp.ones((n, 128), bf)
    heads = []
    for h in range(2):
        off = 64 * (1 - h)
        own = (lane < 64) if h == 0 else (lane >= 64)
        ka_ref[h] = jnp.where(
            own, k, jnp.where(lane < off + 3, one, jnp.where(lane == off + 3, bias, zero))
        )
        q_own = jnp.where(own, q, jnp.where(lane == off + 3, one, zero))
        v_own = jnp.concatenate([jnp.where(own, v, zero), one], axis=1)
        heads.append((off, q_own, v_own))
    causal = lax.broadcasted_iota(jnp.int32, (tile, tile), 1) <= lax.broadcasted_iota(
        jnp.int32, (tile, tile), 0
    )
    lane_t = lane_iota((tile, 128))
    zero_t = jnp.zeros((tile, 128), bf)
    one_t = jnp.ones((tile, 128), bf)
    for i in range(n // tile):
        lo = i * tile
        total = None
        for h in range(2):
            off, q_own, v_own = heads[h]
            q_i = q_own[lo : lo + tile]
            keys = ka_ref[h, : lo + tile]
            scores = jnp.where(causal, dot_nt(q_i, keys[lo:]), masked_score)
            if i:
                scores = jnp.concatenate([dot_nt(q_i, keys[:lo]), scores], axis=1)
            top = jnp.max(scores, axis=1, keepdims=True)
            weights = jnp.exp(scores - top).astype(bf)
            out = dot_nn(weights, v_own[: lo + tile])
            sums = out[:, 128:]
            part = out[:, :128] / sums
            high, mid, low = split3(-(top + jnp.log(sums)))
            own_t = (lane_t < 64) if h == 0 else (lane_t >= 64)
            qa_ref[h, lo : lo + tile] = jnp.where(
                own_t,
                q_i,
                jnp.where(
                    lane_t == off,
                    high,
                    jnp.where(
                        lane_t == off + 1,
                        mid,
                        jnp.where(lane_t == off + 2, low, jnp.where(lane_t == off + 3, one_t, zero_t)),
                    ),
                ),
            )
            total = part if total is None else total + part
        mixed_ref[lo : lo + tile] = total.astype(bf)


def attn_fwd(length, q, k, v, tile):
    n, d = q.shape
    pairs = d // 128
    block = pl.BlockSpec((n, 128), lambda p, length: (0, p))
    wide = pl.BlockSpec((2, n, 128), lambda p, length: (p, 0, 0))

    def attn_forward(*refs):
        attn_fwd_kernel(tile, *refs)

    return pl.pallas_call(
        attn_forward,
        grid_spec=pltpu.PrefetchScalarGridSpec(
            num_scalar_prefetch=1,
            grid=(pairs,),
            in_specs=[block, block, block],
            out_specs=[block, wide, wide],
        ),
        out_shape=[
            jax.ShapeDtypeStruct((n, d), bf),
            jax.ShapeDtypeStruct((2 * pairs, n, 128), bf),
            jax.ShapeDtypeStruct((2 * pairs, n, 128), bf),
        ],
        cost_estimate=pl.CostEstimate(
            flops=12 * n * n * d, bytes_accessed=16 * n * d, transcendentals=n * n * 2 * pairs
        ),
        compiler_params=params(),
    )(length, q, k, v)


def attn_bwd_kernel(tile, qa_ref, ka_ref, v_ref, o_ref, do_ref, dq_ref, dk_ref, dv_ref, dq_sum, va, doa):
    n = v_ref.shape[0]
    lane = lane_iota((n, 128))
    v = v_ref[...]
    do = do_ref[...]
    prod = do.astype(f32) * o_ref[...].astype(f32)
    zero = jnp.zeros((n, 128), bf)
    one = jnp.ones((n, 128), bf)
    for h in range(2):
        own = (lane < 64) if h == 0 else (lane >= 64)
        off = 64 * (1 - h)
        delta = jnp.sum(jnp.where(own, prod, 0.0), axis=1, keepdims=True)
        high, mid, low = split3(jnp.broadcast_to(-delta, (n, 128)))
        va[h] = jnp.where(own, v, jnp.where((lane >= off) & (lane < off + 3), one, zero))
        doa[h] = jnp.where(
            own,
            do,
            jnp.where(
                lane == off,
                high,
                jnp.where(lane == off + 1, mid, jnp.where(lane == off + 2, low, zero)),
            ),
        )
    causal = lax.broadcasted_iota(jnp.int32, (tile, tile), 0) <= lax.broadcasted_iota(
        jnp.int32, (tile, tile), 1
    )
    lane_t = lane_iota((tile, 128))
    zero_t = jnp.zeros((tile, 128), bf)
    for j in range(n // tile):
        lo = j * tile
        dk_sum = None
        dv_sum = None
        for h in range(2):
            k_j = ka_ref[h, lo : lo + tile]
            q_s = qa_ref[h, lo:]
            do_s = doa[h, lo:]
            scores = dot_nt(k_j, q_s)
            near = jnp.where(causal, scores[:, :tile], masked_score)
            scores = jnp.concatenate([near, scores[:, tile:]], axis=1) if lo + tile < n else near
            probs = jnp.exp(scores)
            grad = (probs * dot_nt(va[h, lo : lo + tile], do_s)).astype(bf)
            own_t = (lane_t < 64) if h == 0 else (lane_t >= 64)
            dk = jnp.where(own_t, dot_nn(grad, q_s), 0.0)
            dv = jnp.where(own_t, dot_nn(probs.astype(bf), do_s), 0.0)
            dk_sum = dk if dk_sum is None else dk_sum + dk
            dv_sum = dv if dv_sum is None else dv_sum + dv
            dq = dot_tn(grad, jnp.where(own_t, k_j, zero_t))
            if j == 0 and h == 0:
                dq_sum[...] = dq
            else:
                dq_sum[lo:] += dq
        dk_ref[lo : lo + tile] = dk_sum.astype(bf)
        dv_ref[lo : lo + tile] = dv_sum.astype(bf)
    dq_ref[...] = (dq_sum[...] * (HEAD_DIM**-0.5)).astype(bf)


def attn_bwd(qa, ka, v, o, do, tile):
    n, d = v.shape
    pairs = d // 128
    block = pl.BlockSpec((n, 128), lambda p: (0, p))
    wide = pl.BlockSpec((2, n, 128), lambda p: (p, 0, 0))

    def attn_backward(*refs):
        attn_bwd_kernel(tile, *refs)

    return pl.pallas_call(
        attn_backward,
        grid=(pairs,),
        in_specs=[wide, wide, block, block, block],
        out_specs=[block] * 3,
        out_shape=[jax.ShapeDtypeStruct((n, d), bf)] * 3,
        scratch_shapes=[
            pltpu.VMEM((n, 128), f32),
            pltpu.VMEM((2, n, 128), bf),
            pltpu.VMEM((2, n, 128), bf),
        ],
        cost_estimate=pl.CostEstimate(
            flops=20 * n * n * d, bytes_accessed=20 * n * d, transcendentals=n * n * 2 * pairs
        ),
        compiler_params=params(),
    )(qa, ka, v, o, do)


def weight_copies(i, w_in, w_out, in_buf, out_buf, sem):
    return (
        pltpu.make_async_copy(w_in[i], in_buf.at[i % 2], sem.at[0, i % 2]),
        pltpu.make_async_copy(w_out[i], out_buf.at[i % 2], sem.at[1, i % 2]),
    )


def stream(pieces, copies):
    p = pl.program_id(0)
    for i in range(pieces):

        @pl.when(p == i)
        def _(i=i):
            if i == 0:
                for copy in copies(0):
                    copy.start()
            if i + 1 < pieces:
                for copy in copies(i + 1):
                    copy.start()
            for copy in copies(i):
                copy.wait()


def expert_kernel(pieces, chunk, rows_ref, g_ref, *refs):
    w_in = refs[:pieces]
    w_out = refs[pieces : 2 * pieces]
    act_ref, gp_ref, gm_ref, total, in_buf, out_buf, sem = refs[2 * pieces :]
    p = pl.program_id(0)
    slot = lax.rem(p, 2)
    stream(pieces, lambda i: weight_copies(i, w_in, w_out, in_buf, out_buf, sem))
    for r in range(rows_ref.shape[0] // chunk):
        at = slice(r * chunk, (r + 1) * chunk)
        pre = dot_nn(rows_ref[at], in_buf[slot])
        grad_act = dot_nt(g_ref[at], out_buf[slot])
        half = 0.5 * (1.0 + lax.erf(pre * (0.5**0.5)))
        act_ref[at] = (pre * half).astype(bf)
        density = jnp.exp(-0.5 * pre * pre) * ((2.0 * math.pi) ** -0.5)
        grad_pre = (grad_act * (half + pre * density)).astype(bf)
        gp_ref[at] = grad_pre
        part = dot_nt(grad_pre, in_buf[slot])

        @pl.when(p == 0)
        def _(at=at, part=part):
            total[at] = part

        @pl.when(p > 0)
        def _(at=at, part=part):
            total[at] += part

    @pl.when(p == pieces - 1)
    def _():
        gm_ref[...] = total[...].astype(bf)


def row_chunk(n):
    for parts in (2, 3, 4):
        if n % parts == 0 and (n // parts) % 16 == 0:
            return n // parts
    return n


def expert_main(rows, grads, w_in, w_out):
    n, d = rows.shape
    wide = w_in[0].shape[1]
    pieces = len(w_in)
    full = pl.BlockSpec((n, d), lambda p: (0, 0))
    tile = pl.BlockSpec((n, wide), lambda p: (0, p))
    raw = pl.BlockSpec(memory_space=pl.ANY)
    chunk = row_chunk(n)

    def expert_forward(*refs):
        expert_kernel(pieces, chunk, *refs)

    return pl.pallas_call(
        expert_forward,
        grid=(pieces,),
        in_specs=[full, full] + [raw] * (2 * pieces),
        out_specs=[tile, tile, full],
        out_shape=[jax.ShapeDtypeStruct((n, wide * pieces), bf)] * 2 + [jax.ShapeDtypeStruct((n, d), bf)],
        scratch_shapes=[
            pltpu.VMEM((n, d), f32),
            pltpu.VMEM((2, d, wide), bf),
            pltpu.VMEM((2, wide, d), bf),
            pltpu.SemaphoreType.DMA((2, 2)),
        ],
        cost_estimate=pl.CostEstimate(
            flops=6 * n * d * wide * pieces,
            bytes_accessed=4 * (n + d) * wide * pieces + 6 * n * d,
            transcendentals=2 * n * wide * pieces,
        ),
        compiler_params=params(),
    )(rows, grads, *w_in, *w_out)


def expert_result(acts, w_out, experts):
    n = acts[0].shape[0]
    wide, d = w_out[0].shape
    pieces, parts = len(w_out), len(acts)
    each = n // experts

    def expert_outputs(*refs):
        act = refs[:parts]
        w = refs[parts : parts + pieces]
        out_ref, total, buf, sem = refs[parts + pieces :]
        p = pl.program_id(0)
        slot = lax.rem(p, 2)
        stream(pieces, lambda i: (pltpu.make_async_copy(w[i], buf.at[i % 2], sem.at[i % 2]),))
        for h in range(parts):
            part = dot_nn(act[h][...], buf[slot])

            @pl.when(p == 0)
            def _(h=h, part=part):
                total[h] = part

            @pl.when(p > 0)
            def _(h=h, part=part):
                total[h] += part

        @pl.when(p == pieces - 1)
        def _():
            if parts == 1:
                out_ref[...] = total[0].astype(bf)
            else:
                for e in range(experts):
                    for h in range(parts):
                        at = (e * parts + h) * each
                        out_ref[at : at + each] = total[h, e * each : (e + 1) * each].astype(bf)

    return pl.pallas_call(
        expert_outputs,
        grid=(pieces,),
        in_specs=[pl.BlockSpec((n, wide), lambda p: (0, p))] * parts
        + [pl.BlockSpec(memory_space=pl.ANY)] * pieces,
        out_specs=pl.BlockSpec((n * parts, d), lambda p: (0, 0)),
        out_shape=jax.ShapeDtypeStruct((n * parts, d), bf),
        scratch_shapes=[
            pltpu.VMEM((parts, n, d), f32),
            pltpu.VMEM((2, wide, d), bf),
            pltpu.SemaphoreType.DMA((2,)),
        ],
        cost_estimate=pl.CostEstimate(
            flops=2 * n * parts * d * wide * pieces,
            bytes_accessed=2 * (n * parts + d) * wide * pieces + 2 * n * parts * d,
            transcendentals=0,
        ),
        compiler_params=params(),
    )(*acts, *w_out)


def expert_weights(lefts, rights, pieces, split_left):
    parts = len(lefts)
    half = pieces // 2
    n = lefts[0].shape[0]
    wide = (lefts if split_left else rights)[0].shape[1] // pieces
    d = (rights if split_left else lefts)[0].shape[1]
    full = pl.BlockSpec((n, d), lambda p: (0, 0))
    tile = pl.BlockSpec((n, wide), lambda p: (0, p))
    shape = (wide, d) if split_left else (d, wide)

    def expert_weight_grads(*refs):
        near_ref, far_ref = refs[2 * parts :]
        total = sum(dot_tn(refs[h][...], refs[parts + h][...]) for h in range(parts)).astype(bf)
        p = pl.program_id(0)

        @pl.when(p < half)
        def _():
            near_ref[0] = total

        @pl.when(p >= half)
        def _():
            far_ref[0] = total

    return pl.pallas_call(
        expert_weight_grads,
        grid=(pieces,),
        in_specs=[tile if split_left else full] * parts + [full if split_left else tile] * parts,
        out_specs=[
            pl.BlockSpec((1,) + shape, lambda p: (jnp.minimum(p, half - 1), 0, 0)),
            pl.BlockSpec((1,) + shape, lambda p: (jnp.maximum(p - half, 0), 0, 0)),
        ],
        out_shape=[jax.ShapeDtypeStruct((half,) + shape, bf)] * 2,
        cost_estimate=pl.CostEstimate(
            flops=2 * n * parts * d * wide * pieces,
            bytes_accessed=2 * (n * parts + d) * wide * pieces + 2 * n * parts * d,
            transcendentals=0,
        ),
        compiler_params=params(),
    )(*lefts, *rights)


def picks(rows, columns, target, axis):
    at = lax.broadcasted_iota(jnp.int32, (rows, columns), axis)
    return (at == target).astype(f32).astype(bf)


def place(target, x_ref, outs):
    for h, out_ref in enumerate(outs):
        slots = out_ref.shape[0]
        pick = picks(slots, x_ref.shape[0], target - h * slots, 0)
        out_ref[...] = dot_nn(pick, x_ref[...]).astype(bf)


def fetch(target, parts):
    total = None
    for h, y_ref in enumerate(parts):
        slots = y_ref.shape[0]
        got = dot_nn(picks(target.shape[0], slots, target - h * slots, 1), y_ref[...])
        total = got if total is None else total + got
    return total


def place_rows(target_row, x, slots, parts):
    n, d = x.shape

    def rows_to_slots(target_ref, x_ref, *outs):
        place(target_ref[...], x_ref, outs)

    return pl.pallas_call(
        rows_to_slots,
        out_shape=[jax.ShapeDtypeStruct((slots // parts, d), bf)] * parts,
        cost_estimate=pl.CostEstimate(
            flops=2 * n * d * slots, bytes_accessed=2 * (n + slots) * d, transcendentals=0
        ),
        compiler_params=params(),
    )(target_row, x)


def each_chunk(n, body):
    step = 256 if n % 256 == 0 else n

    @pl.loop(0, n // step)
    def _(i):
        body(pl.ds(pl.multiple_of(i * step, step), step))


def add_rows(target_col, returned, hidden):
    n, d = hidden.shape

    def block_outputs(target_ref, y_ref, hid_ref, out_ref):
        def body(at):
            out_ref[at] = (hid_ref[at] + fetch(target_ref[at], [y_ref])).astype(bf)

        each_chunk(n, body)

    return pl.pallas_call(
        block_outputs,
        out_shape=jax.ShapeDtypeStruct((n, d), bf),
        cost_estimate=pl.CostEstimate(
            flops=2 * n * d * returned.shape[0], bytes_accessed=10 * n * d, transcendentals=0
        ),
        compiler_params=params(),
    )(target_col, returned, hidden)


def centred_rows(values):
    centre = jnp.mean(values, axis=-1, keepdims=True)
    centred = values - centre
    spread = jnp.mean(centred * centred, axis=-1, keepdims=True)
    return centred, lax.rsqrt(spread + eps)


def norm_grad(values, gain, grad):
    centred, inverse = centred_rows(values)
    unit = centred * inverse
    g = gain * grad
    back = (g - jnp.mean(g, axis=-1, keepdims=True) - unit * jnp.mean(g * unit, axis=-1, keepdims=True)) * inverse
    return back, jnp.sum(grad * unit, axis=0, keepdims=True), jnp.sum(grad, axis=0, keepdims=True)


def projections(place_a, place_b, arrays_a, arrays_b, tokens, rows_in, rows_out, near):
    n, d = tokens.shape
    count = place_a.shape[0]
    rest = rows_in - near
    sources = len(arrays_a)
    per = count // sources

    def norm_and_projections(at_a, at_b, tok_ref, *refs):
        a_refs = refs[:sources]
        b_refs = refs[sources : 2 * sources]
        in_ref, out_ref, norm_ref, normed_ref, q_ref, k_ref, v_ref, norm_buf, sem = refs[2 * sources :]
        norm_copies = []
        copies = []
        for s in range(count):
            a, b = a_refs[s // per], b_refs[s // per]
            norm_copies.append(
                pltpu.make_async_copy(b.at[s % per, pl.ds(rest + rows_out, 8)], norm_buf.at[s], sem.at[3, s])
            )
            to_a = pl.multiple_of(at_a[s] * rows_in, 8)
            to_b = pl.multiple_of(at_b[s] * rows_in + near, 8)
            to_out = pl.multiple_of(at_b[s] * rows_out, 8)
            copies.append(
                pltpu.make_async_copy(a.at[s % per], in_ref.at[pl.ds(to_a, near)], sem.at[0, s])
            )
            copies.append(
                pltpu.make_async_copy(b.at[s % per, pl.ds(0, rest)], in_ref.at[pl.ds(to_b, rest)], sem.at[1, s])
            )
            copies.append(
                pltpu.make_async_copy(
                    b.at[s % per, pl.ds(rest, rows_out)], out_ref.at[pl.ds(to_out, rows_out)], sem.at[2, s]
                )
            )
        for copy in norm_copies + copies:
            copy.start()
        for copy in norm_copies:
            copy.wait()
        norm_ref[...] = jnp.sum(norm_buf[...].astype(f32), axis=0)

        def norm(at):
            centred, inverse = centred_rows(tok_ref[at].astype(f32))
            normed_ref[at] = (centred * inverse * norm_ref[0:1] + norm_ref[2:3]).astype(bf)

        each_chunk(n, norm)
        for copy in copies:
            copy.wait()

        def project(at):
            x = normed_ref[at]
            for i, ref in enumerate((q_ref, k_ref, v_ref)):
                ref[at] = dot_nn(x, in_ref[i * d : (i + 1) * d]).astype(bf)

        each_chunk(n, project)

    vm = pl.BlockSpec(memory_space=pltpu.VMEM)
    sm = pl.BlockSpec(memory_space=pltpu.SMEM)
    raw = pl.BlockSpec(memory_space=pl.ANY)
    return pl.pallas_call(
        norm_and_projections,
        in_specs=[sm, sm, vm] + [raw] * (2 * sources),
        out_specs=[vm] * 7,
        out_shape=[
            jax.ShapeDtypeStruct((count * rows_in, d), bf),
            jax.ShapeDtypeStruct((count * rows_out, d), bf),
            jax.ShapeDtypeStruct((8, d), f32),
        ]
        + [jax.ShapeDtypeStruct((n, d), bf)] * 4,
        scratch_shapes=[pltpu.VMEM((count, 8, d), bf), pltpu.SemaphoreType.DMA((4, count))],
        cost_estimate=pl.CostEstimate(
            flops=6 * n * d * d, bytes_accessed=4 * count * (rows_in + rows_out) * d + 10 * n * d, transcendentals=n
        ),
        compiler_params=params(),
    )(place_a, place_b, tokens, *arrays_a, *arrays_b)


def mix_and_place(target_row, tokens, mixed, all_out, norms, slots, parts):
    n, d = tokens.shape

    def mix_and_norm(target_ref, tok_ref, mixed_ref, w_ref, norm_ref, hid_ref, *refs):
        rows = refs[parts]

        def body(at):
            hidden = tok_ref[at].astype(f32) + dot_nn(mixed_ref[at], w_ref[...])
            hid_ref[at] = hidden
            centred, inverse = centred_rows(hidden)
            rows[at] = (centred * inverse * norm_ref[1:2] + norm_ref[3:4]).astype(bf)

        each_chunk(n, body)
        place(target_ref[...], rows, refs[:parts])

    return pl.pallas_call(
        mix_and_norm,
        out_shape=[jax.ShapeDtypeStruct((n, d), f32)]
        + [jax.ShapeDtypeStruct((slots // parts, d), bf)] * parts,
        scratch_shapes=[pltpu.VMEM((n, d), bf)],
        cost_estimate=pl.CostEstimate(
            flops=2 * n * d * (d + slots), bytes_accessed=8 * n * d + 2 * slots * d + 2 * d * d, transcendentals=n
        ),
        compiler_params=params(),
    )(target_row, tokens, mixed, all_out, norms)


def split_groups(core_ref, total, away_ref, own_ref):
    columns, rows = away_ref.shape[0], away_ref.shape[1]
    core = core_ref[0]
    for y in range(columns):
        away = pl.multiple_of((2 * y + 1 - core) * rows, 8)
        own = pl.multiple_of((2 * y + core) * rows, 8)
        away_ref[y] = total[pl.ds(away, rows)].astype(bf)
        own_ref[y] = total[pl.ds(own, rows)].astype(bf)


def norm_back(core, target_col, backs, hidden, cotangent, mixed, all_out, norms, columns):
    n, d = hidden.shape
    parts = len(backs)
    rows = d // (2 * columns)

    def second_norm_back(core_ref, target_ref, *refs):
        back_refs = refs[:parts]
        hid_ref, cot_ref, mixed_ref, w_ref, norm_ref = refs[parts : parts + 5]
        gh_ref, gm_ref, sum_ref, away_ref, own_ref, low, total = refs[parts + 5 :]
        sum_ref[...] = jnp.zeros_like(sum_ref)

        def body(at):
            grad = fetch(target_ref[at], back_refs)
            back, gain, bias = norm_grad(hid_ref[at], norm_ref[1:2], grad)
            grad_hidden = cot_ref[at].astype(f32) + back
            gh_ref[at] = grad_hidden
            sum_ref[0:1] += gain
            sum_ref[1:2] += bias
            low[at] = grad_hidden.astype(bf)
            gm_ref[at] = dot_nt(low[at], w_ref[...]).astype(bf)

        each_chunk(n, body)
        total[...] = dot_tn(mixed_ref[...], low[...])
        split_groups(core_ref, total, away_ref, own_ref)

    sm = pl.BlockSpec(memory_space=pltpu.SMEM)
    vm = pl.BlockSpec(memory_space=pltpu.VMEM)
    return pl.pallas_call(
        second_norm_back,
        in_specs=[sm] + [vm] * (6 + parts),
        out_specs=[vm] * 5,
        out_shape=[
            jax.ShapeDtypeStruct((n, d), f32),
            jax.ShapeDtypeStruct((n, d), bf),
            jax.ShapeDtypeStruct((8, d), f32),
            jax.ShapeDtypeStruct((columns, rows, d), bf),
            jax.ShapeDtypeStruct((columns, rows, d), bf),
        ],
        scratch_shapes=[pltpu.VMEM((n, d), bf), pltpu.VMEM((d, d), f32)],
        cost_estimate=pl.CostEstimate(
            flops=6 * n * d * d, bytes_accessed=16 * n * d + 4 * d * d, transcendentals=n
        ),
        compiler_params=params(),
    )(core, target_col, *backs, hidden, cotangent, mixed, all_out, norms)


def projection_grads(core, normed, grads, columns):
    n, d = normed.shape
    rows = 3 * d // (2 * columns)

    def projection_weight_grads(core_ref, x_ref, *refs):
        away_ref, own_ref, total = refs[3:]
        for i in range(3):
            total[i * d : (i + 1) * d] = dot_tn(x_ref[...], refs[i][...])
        split_groups(core_ref, total, away_ref, own_ref)

    sm = pl.BlockSpec(memory_space=pltpu.SMEM)
    vm = pl.BlockSpec(memory_space=pltpu.VMEM)
    return pl.pallas_call(
        projection_weight_grads,
        in_specs=[sm] + [vm] * 4,
        out_specs=[vm] * 2,
        out_shape=[jax.ShapeDtypeStruct((columns, rows, grads[0].shape[1]), bf)] * 2,
        scratch_shapes=[pltpu.VMEM((3 * d, grads[0].shape[1]), f32)],
        cost_estimate=pl.CostEstimate(
            flops=6 * n * d * d, bytes_accessed=8 * n * d + 6 * d * d, transcendentals=0
        ),
        compiler_params=params(),
    )(core, normed, *grads)


def first_norm_back(grads, all_in, tokens, norms, grad_hidden):
    n, d = tokens.shape

    def input_grads(q_ref, k_ref, v_ref, w_ref, tok_ref, norm_ref, gh_ref, out_ref, sum_ref):
        sum_ref[...] = jnp.zeros_like(sum_ref)

        def body(at):
            grad = dot_nt(q_ref[at], w_ref[0:d])
            grad += dot_nt(k_ref[at], w_ref[d : 2 * d])
            grad += dot_nt(v_ref[at], w_ref[2 * d :])
            back, gain, bias = norm_grad(tok_ref[at].astype(f32), norm_ref[0:1], grad)
            out_ref[at] = gh_ref[at] + back
            sum_ref[0:1] += gain
            sum_ref[1:2] += bias

        each_chunk(n, body)

    return pl.pallas_call(
        input_grads,
        out_shape=[jax.ShapeDtypeStruct((n, d), f32), jax.ShapeDtypeStruct((8, d), f32)],
        cost_estimate=pl.CostEstimate(
            flops=6 * n * d * d, bytes_accessed=16 * n * d + 6 * d * d, transcendentals=n
        ),
        compiler_params=params(),
    )(*grads, all_in, tokens, norms, grad_hidden)


def from_others(x, axis):
    n = lax.axis_size(axis)
    return [x] + [lax.ppermute(x, axis, [(i, (i - s) % n) for i in range(n)]) for s in range(1, n)]


def gather_stage(x, axis):
    return jnp.stack(from_others(x, axis))


def block_places(order, sizes):
    place = jnp.arange(math.prod(sizes.values()), dtype=jnp.int32)
    where = {}
    step = 1
    for axis in order:
        where[axis] = (place // step + lax.axis_index(axis)) % sizes[axis]
        step *= sizes[axis]
    whole = 0
    for axis in EVERY:
        whole = whole * sizes[axis] + where[axis]
    return whole.astype(jnp.int32)


def gather_parameters(attn_in, attn_out, ln_gain, ln_bias, tokens, during):
    rows_in, d = attn_in.shape
    rows_out = attn_out.shape[0]
    span = ln_gain.shape[1]
    sizes = {axis: lax.axis_size(axis) for axis in EVERY}
    count = math.prod(sizes.values())
    me = lax.axis_index(EVERY)
    own = jnp.concatenate([ln_gain, ln_bias], axis=0)
    norm = jnp.where(lane_iota((4, d)) // span == me, jnp.tile(own, (1, count)), 0)
    norm = jnp.pad(norm, ((0, 4), (0, 0)))
    if rows_in % 8 or rows_out % 8:
        whole_in, whole_out = [lax.all_gather(a, EVERY, axis=0, tiled=True) for a in (attn_in, attn_out)]
        whole_norm = lax.all_gather(norm, EVERY, axis=0, tiled=False)
        at = jnp.arange(1, dtype=jnp.int32)
        near = 3 * d // 16 * 8
        second = jnp.concatenate([whole_in[near:], whole_out, jnp.sum(whole_norm.astype(f32), axis=0).astype(bf)])
        return projections(at, at, [whole_in[None, :near]], [second[None]], tokens, 3 * d, d, near), during
    near = 56 if rows_in == 72 else rows_in // 16 * 8
    b = jnp.concatenate([attn_in[near:], attn_out, norm], axis=0)
    order_a = ("z", "x", "y", "core")
    order_b = ("y", "z", "x", "core")
    a = gather_stage(attn_in[:near], "z")
    a, during = lax.optimization_barrier((a, during))
    b = gather_stage(b, "y")
    a = gather_stage(a, "x")
    b = gather_stage(b, "z")
    a = gather_stage(a, "y")
    b = gather_stage(b, "x")
    a = a.reshape(count // 2, near, d)
    b = b.reshape(count // 2, -1, d)
    out = projections(
        block_places(order_a, sizes),
        block_places(order_b, sizes),
        from_others(a, "core"),
        from_others(b, "core"),
        tokens,
        rows_in,
        rows_out,
        near,
    )
    return out, during


def other_core(x):
    return lax.ppermute(x, "core", [(0, 1), (1, 0)])


def scatter_pieces(near, far):
    columns = near.shape[0]
    other = other_core(far)
    total = near[0].astype(f32) + other[0].astype(f32)
    for s in range(1, columns):
        pair = (near[s].astype(f32) + other[s].astype(f32)).astype(bf)
        moved = lax.ppermute(pair, "y", [(i, (i + s) % columns) for i in range(columns)])
        total = total + moved.astype(f32)
    return total


def scatter_rows(away, own):
    columns, rows, d = own.shape
    ring = lax.axis_size("z") * lax.axis_size("x")
    pair = (own.astype(f32) + other_core(away).astype(f32)).astype(bf)
    moved = lax.all_to_all(
        pair.reshape(columns * ring, rows // ring, d), RING, split_axis=0, concat_axis=0, tiled=True
    )
    return jnp.sum(moved.astype(f32), axis=0)


def scatter_norms(terms):
    pair = terms + other_core(terms)
    columns = lax.axis_size("y")
    ring = lax.axis_size("z") * lax.axis_size("x")
    span = terms.shape[1] // (2 * columns * ring)
    pair = pair.reshape(4, columns, 2, ring, span)
    mine = lax.dynamic_index_in_dim(pair, lax.axis_index("core"), 2, keepdims=False)
    mine = mine.transpose(1, 2, 0, 3).reshape(columns * ring, 4 * span)
    high = mine.astype(bf)
    low = (mine - high.astype(f32)).astype(bf)
    both = jnp.stack([high, low], axis=1)
    both = jnp.pad(both, ((0, 0), (0, 6), (0, -4 * span % 128)))
    moved = lax.all_to_all(both, RING, split_axis=0, concat_axis=0, tiled=True)
    return jnp.sum(moved[:, :2, : 4 * span].astype(f32), axis=(0, 1)).reshape(4, span)


def swap(x, experts):
    n, d = x.shape
    moved = lax.all_to_all(
        x.reshape(experts, n // experts, d), EXPERT, split_axis=0, concat_axis=0, tiled=True
    )
    return moved.reshape(n, d)


def shards(tokens, lengths, routes, attn_in, attn_out, ln_gain, ln_bias, w_in, w_out, cotangent):
    row_count, d = tokens.shape
    limit = lengths[0]
    columns = lax.axis_size("y")
    experts = lax.axis_size("z") * lax.axis_size("x")
    capacity = max(2, 9 * row_count // (8 * experts))
    slot_total = experts * capacity
    parts = 2 if capacity % 16 == 0 else 1
    share = capacity // parts
    core = lax.axis_index("core").astype(jnp.int32)[None]

    valid = jnp.arange(row_count) < limit
    onehot = ((routes[:, None] == jnp.arange(experts)[None, :]) & valid[:, None]).astype(jnp.int32)
    ranks = jnp.sum((jnp.cumsum(onehot, axis=0) - 1) * onehot, axis=1)
    target = jnp.where(valid, routes * capacity + ranks, 2 * slot_total)
    cut = jnp.where(
        valid, ranks // share * (experts * share) + routes * share + ranks % share, 2 * slot_total
    )
    cut_row, cut_col = cut[None, :], cut[:, None]

    placed = place_rows(cut_row, cotangent, slot_total, parts)
    gathered, placed = gather_parameters(attn_in, attn_out, ln_gain, ln_bias, tokens, placed)
    all_in, all_out, norms, normed, query, key_rows, value_rows = gathered
    grads = [swap(x, experts) for x in placed]
    in_near = from_others(w_in[0], "y")
    out_near = from_others(w_out[0], "y")

    tile = min(256, row_count)
    mixed, query_wide, key_wide = attn_fwd(lengths, query, key_rows, value_rows, tile)
    mixed, in_near, out_near = lax.optimization_barrier((mixed, in_near, out_near))
    in_pieces = in_near + [other_core(x) for x in in_near]
    out_pieces = out_near + [other_core(x) for x in out_near]
    hidden, *sends = mix_and_place(cut_row, tokens, mixed, all_out, norms, slot_total, parts)

    acts, grad_pres, rows, backs = [], [], [], []
    for h in range(parts):
        rows.append(swap(sends[h], experts))
        act, grad_pre, grad_moe = expert_main(rows[h], grads[h], in_pieces, out_pieces)
        acts.append(act)
        grad_pres.append(grad_pre)
        backs.append(swap(grad_moe, experts))
    grad_w_in = scatter_pieces(*expert_weights(rows, grad_pres, len(in_pieces), False))
    grad_w_out = scatter_pieces(*expert_weights(acts, grads, len(in_pieces), True))
    returned = swap(expert_result(acts, out_pieces, experts), experts)

    grad_hidden, grad_mixed, sums_second, away, own = norm_back(
        core, cut_col, backs, hidden, cotangent, mixed, all_out, norms, columns
    )
    grad_attn_out = scatter_rows(away, own)
    grads_qkv = attn_bwd(query_wide, key_wide, value_rows, mixed, grad_mixed, tile)
    away, own = projection_grads(core, normed, grads_qkv, columns)
    grad_attn_in = scatter_rows(away, own)
    grad_tokens, sums_first = first_norm_back(grads_qkv, all_in, tokens, norms, grad_hidden)
    norm_sums = scatter_norms(
        jnp.concatenate([sums_first[:1], sums_second[:1], sums_first[1:2], sums_second[1:2]], axis=0)
    )
    returned, unused = lax.optimization_barrier((returned, sums_first))
    block_out = add_rows(target[:, None], returned, hidden)
    return (
        block_out,
        grad_tokens,
        grad_attn_in,
        grad_attn_out,
        norm_sums[:2],
        norm_sums[2],
        norm_sums[3],
        grad_w_in[None],
        grad_w_out[None],
    )


def solution(mesh):
    columns, experts = mesh.devices.shape
    across = 1
    while (2 * across) ** 2 <= experts:
        across *= 2
    fine = Mesh(mesh.devices.reshape(columns // 2, 2, experts // across, across), EVERY)
    every = P(EVERY)
    dp = ("y", "core")
    in_specs = (
        P(EVERY, None),
        every,
        every,
        P(EVERY, None),
        P(EVERY, None),
        P(None, EVERY),
        P(None, EVERY),
        P(EXPERT, None, dp),
        P(EXPERT, dp, None),
        P(EVERY, None),
    )
    out_specs = (
        P(EVERY, None),
        P(EVERY, None),
        P(EVERY, None),
        P(EVERY, None),
        P(None, EVERY),
        every,
        every,
        P(EXPERT, None, dp),
        P(EXPERT, dp, None),
    )
    return jax.shard_map(shards, mesh=fine, in_specs=in_specs, out_specs=out_specs, check_vma=False)
```

```python
import math
import jax
import jax.numpy as jnp
from jax import lax
from jax.experimental import pallas as pl
from jax.experimental.pallas import tpu as pltpu
from jax.sharding import Mesh
from jax.sharding import PartitionSpec as P

HEADS = 12
HEAD_DIM = 64
eps = 1e-05
masked_score = -1e30
bf = jnp.bfloat16
f32 = jnp.float32
VMEM_LIMIT = 60 << 20
EVERY = ("y", "core", "z", "x")
RING = ("y", "z", "x")
EXPERT = ("z", "x")


def dot_nt(left, right):
    return lax.dot_general(left, right, (((1,), (1,)), ((), ())), preferred_element_type=f32)


def dot_nn(left, right):
    return lax.dot_general(left, right, (((1,), (0,)), ((), ())), preferred_element_type=f32)


def dot_tn(left, right):
    return lax.dot_general(left, right, (((0,), (0,)), ((), ())), preferred_element_type=f32)


def params(**kw):
    return pltpu.CompilerParams(vmem_limit_bytes=VMEM_LIMIT, **kw)


def split3(x):
    high = x.astype(bf)
    rest = x - high.astype(f32)
    mid = rest.astype(bf)
    return high, mid, (rest - mid.astype(f32)).astype(bf)


def lane_iota(shape):
    return lax.broadcasted_iota(jnp.int32, shape, len(shape) - 1)


def attn_fwd_kernel(tile, len_ref, q_ref, k_ref, v_ref, mixed_ref, qa_ref, ka_ref):
    n = q_ref.shape[0]
    lane = lane_iota((n, 128))
    key_pos = lax.broadcasted_iota(jnp.int32, (n, 128), 0)
    bias = jnp.where(key_pos < len_ref[0], 0.0, masked_score).astype(bf)
    q = q_ref[...] * bf(HEAD_DIM**-0.5)
    k = k_ref[...]
    v = v_ref[...]
    zero = jnp.zeros((n, 128), bf)
    one = jnp.ones((n, 128), bf)
    heads = []
    for h in range(2):
        off = 64 * (1 - h)
        own = (lane < 64) if h == 0 else (lane >= 64)
        ka_ref[h] = jnp.where(
            own, k, jnp.where(lane < off + 3, one, jnp.where(lane == off + 3, bias, zero))
        )
        q_own = jnp.where(own, q, jnp.where(lane == off + 3, one, zero))
        v_own = jnp.concatenate([jnp.where(own, v, zero), one], axis=1)
        heads.append((off, q_own, v_own))
    causal = lax.broadcasted_iota(jnp.int32, (tile, tile), 1) <= lax.broadcasted_iota(
        jnp.int32, (tile, tile), 0
    )
    lane_t = lane_iota((tile, 128))
    zero_t = jnp.zeros((tile, 128), bf)
    one_t = jnp.ones((tile, 128), bf)
    for i in range(n // tile):
        lo = i * tile
        total = None
        for h in range(2):
            off, q_own, v_own = heads[h]
            q_i = q_own[lo : lo + tile]
            keys = ka_ref[h, : lo + tile]
            scores = jnp.where(causal, dot_nt(q_i, keys[lo:]), masked_score)
            if i:
                scores = jnp.concatenate([dot_nt(q_i, keys[:lo]), scores], axis=1)
            top = jnp.max(scores, axis=1, keepdims=True)
            weights = jnp.exp(scores - top).astype(bf)
            out = dot_nn(weights, v_own[: lo + tile])
            sums = out[:, 128:]
            part = out[:, :128] / sums
            high, mid, low = split3(-(top + jnp.log(sums)))
            own_t = (lane_t < 64) if h == 0 else (lane_t >= 64)
            qa_ref[h, lo : lo + tile] = jnp.where(
                own_t,
                q_i,
                jnp.where(
                    lane_t == off,
                    high,
                    jnp.where(
                        lane_t == off + 1,
                        mid,
                        jnp.where(lane_t == off + 2, low, jnp.where(lane_t == off + 3, one_t, zero_t)),
                    ),
                ),
            )
            total = part if total is None else total + part
        mixed_ref[lo : lo + tile] = total.astype(bf)


def attn_fwd(length, q, k, v, tile):
    n, d = q.shape
    pairs = d // 128
    block = pl.BlockSpec((n, 128), lambda p, length: (0, p))
    wide = pl.BlockSpec((2, n, 128), lambda p, length: (p, 0, 0))

    def attn_forward(*refs):
        attn_fwd_kernel(tile, *refs)

    return pl.pallas_call(
        attn_forward,
        grid_spec=pltpu.PrefetchScalarGridSpec(
            num_scalar_prefetch=1,
            grid=(pairs,),
            in_specs=[block, block, block],
            out_specs=[block, wide, wide],
        ),
        out_shape=[
            jax.ShapeDtypeStruct((n, d), bf),
            jax.ShapeDtypeStruct((2 * pairs, n, 128), bf),
            jax.ShapeDtypeStruct((2 * pairs, n, 128), bf),
        ],
        cost_estimate=pl.CostEstimate(
            flops=12 * n * n * d, bytes_accessed=16 * n * d, transcendentals=n * n * 2 * pairs
        ),
        compiler_params=params(),
    )(length, q, k, v)


def attn_bwd_kernel(tile, qa_ref, ka_ref, v_ref, o_ref, do_ref, dq_ref, dk_ref, dv_ref, dq_sum, va, doa):
    n = v_ref.shape[0]
    lane = lane_iota((n, 128))
    v = v_ref[...]
    do = do_ref[...]
    prod = do.astype(f32) * o_ref[...].astype(f32)
    zero = jnp.zeros((n, 128), bf)
    one = jnp.ones((n, 128), bf)
    for h in range(2):
        own = (lane < 64) if h == 0 else (lane >= 64)
        off = 64 * (1 - h)
        delta = jnp.sum(jnp.where(own, prod, 0.0), axis=1, keepdims=True)
        high, mid, low = split3(jnp.broadcast_to(-delta, (n, 128)))
        va[h] = jnp.where(own, v, jnp.where((lane >= off) & (lane < off + 3), one, zero))
        doa[h] = jnp.where(
            own,
            do,
            jnp.where(
                lane == off,
                high,
                jnp.where(lane == off + 1, mid, jnp.where(lane == off + 2, low, zero)),
            ),
        )
    causal = lax.broadcasted_iota(jnp.int32, (tile, tile), 0) <= lax.broadcasted_iota(
        jnp.int32, (tile, tile), 1
    )
    lane_t = lane_iota((tile, 128))
    zero_t = jnp.zeros((tile, 128), bf)
    for j in range(n // tile):
        lo = j * tile
        dk_sum = None
        dv_sum = None
        for h in range(2):
            k_j = ka_ref[h, lo : lo + tile]
            q_s = qa_ref[h, lo:]
            do_s = doa[h, lo:]
            scores = dot_nt(k_j, q_s)
            near = jnp.where(causal, scores[:, :tile], masked_score)
            scores = jnp.concatenate([near, scores[:, tile:]], axis=1) if lo + tile < n else near
            probs = jnp.exp(scores)
            grad = (probs * dot_nt(va[h, lo : lo + tile], do_s)).astype(bf)
            own_t = (lane_t < 64) if h == 0 else (lane_t >= 64)
            dk = jnp.where(own_t, dot_nn(grad, q_s), 0.0)
            dv = jnp.where(own_t, dot_nn(probs.astype(bf), do_s), 0.0)
            dk_sum = dk if dk_sum is None else dk_sum + dk
            dv_sum = dv if dv_sum is None else dv_sum + dv
            dq = dot_tn(grad, jnp.where(own_t, k_j, zero_t))
            if j == 0 and h == 0:
                dq_sum[...] = dq
            else:
                dq_sum[lo:] += dq
        dk_ref[lo : lo + tile] = dk_sum.astype(bf)
        dv_ref[lo : lo + tile] = dv_sum.astype(bf)
    dq_ref[...] = (dq_sum[...] * (HEAD_DIM**-0.5)).astype(bf)


def attn_bwd(qa, ka, v, o, do, tile):
    n, d = v.shape
    pairs = d // 128
    block = pl.BlockSpec((n, 128), lambda p: (0, p))
    wide = pl.BlockSpec((2, n, 128), lambda p: (p, 0, 0))

    def attn_backward(*refs):
        attn_bwd_kernel(tile, *refs)

    return pl.pallas_call(
        attn_backward,
        grid=(pairs,),
        in_specs=[wide, wide, block, block, block],
        out_specs=[block] * 3,
        out_shape=[jax.ShapeDtypeStruct((n, d), bf)] * 3,
        scratch_shapes=[
            pltpu.VMEM((n, 128), f32),
            pltpu.VMEM((2, n, 128), bf),
            pltpu.VMEM((2, n, 128), bf),
        ],
        cost_estimate=pl.CostEstimate(
            flops=20 * n * n * d, bytes_accessed=20 * n * d, transcendentals=n * n * 2 * pairs
        ),
        compiler_params=params(),
    )(qa, ka, v, o, do)


def weight_copies(i, w_in, w_out, in_buf, out_buf, sem):
    return (
        pltpu.make_async_copy(w_in[i], in_buf.at[i % 2], sem.at[0, i % 2]),
        pltpu.make_async_copy(w_out[i], out_buf.at[i % 2], sem.at[1, i % 2]),
    )


def stream(pieces, copies):
    p = pl.program_id(0)
    for i in range(pieces):

        @pl.when(p == i)
        def _(i=i):
            if i == 0:
                for copy in copies(0):
                    copy.start()
            if i + 1 < pieces:
                for copy in copies(i + 1):
                    copy.start()
            for copy in copies(i):
                copy.wait()


def expert_group(order, first, blocks, grads, w_in, w_out, kept, total_rows):
    each, d = blocks[0].shape
    count, pieces = len(blocks), len(w_in)
    n = each * count
    wide = w_in[0].shape[1]
    chunk = row_chunk(n)
    carried = len(kept) if kept else 0

    def expert_forward(order_ref, *refs):
        block_refs = refs[:count]
        g_ref = refs[count]
        wi = refs[count + 1 : count + 1 + pieces]
        wo = refs[count + 1 + pieces : count + 1 + 2 * pieces]
        outs = refs[count + 1 + 2 * pieces + carried :]
        act_ref, gp_ref, rows_ref, grads_ref = outs[:4]
        gm_refs = outs[4 : 4 + count]
        total, in_buf, out_buf, sem = outs[4 + count :]
        p = pl.program_id(0)
        slot = lax.rem(p, 2)

        @pl.when(p == 0)
        def _():
            for k in range(count):
                rows_ref[k * each : (k + 1) * each] = block_refs[k][...]
                grads_ref[k * each : (k + 1) * each] = g_ref[order_ref[first + k]]

        stream(pieces, lambda i: weight_copies(i, wi, wo, in_buf, out_buf, sem))
        for r in range(n // chunk):
            at = slice(r * chunk, (r + 1) * chunk)
            pre = dot_nn(rows_ref[at], in_buf[slot])
            grad_act = dot_nt(grads_ref[at], out_buf[slot])
            half = 0.5 * (1.0 + lax.erf(pre * (0.5**0.5)))
            act_ref[at] = (pre * half).astype(bf)
            density = jnp.exp(-0.5 * pre * pre) * ((2.0 * math.pi) ** -0.5)
            grad_pre = (grad_act * (half + pre * density)).astype(bf)
            gp_ref[at] = grad_pre
            part = dot_nt(grad_pre, in_buf[slot])

            @pl.when(p == 0)
            def _(at=at, part=part):
                total[at] = part

            @pl.when(p > 0)
            def _(at=at, part=part):
                total[at] += part

        @pl.when(p == pieces - 1)
        def _():
            for k in range(count):
                gm_refs[k][...] = total[k * each : (k + 1) * each].astype(bf)

    place = first // count
    raw = pl.BlockSpec(memory_space=pl.ANY)
    tile = pl.BlockSpec((n, wide), lambda p: (place, p))
    rows = pl.BlockSpec((n, d), lambda p: (place, 0))
    one = pl.BlockSpec((each, d), lambda p: (0, 0))
    whole = pl.BlockSpec(grads.shape, lambda p: (0, 0, 0))
    base = 2 + count + 2 * pieces
    out = pl.pallas_call(
        expert_forward,
        grid=(pieces,),
        in_specs=[pl.BlockSpec(memory_space=pltpu.SMEM)]
        + [one] * count
        + [whole]
        + [raw] * (2 * pieces + carried),
        out_specs=[tile, tile, rows, rows] + [one] * count,
        out_shape=[jax.ShapeDtypeStruct((total_rows, wide * pieces), bf)] * 2
        + [jax.ShapeDtypeStruct((total_rows, d), bf)] * 2
        + [jax.ShapeDtypeStruct((each, d), bf)] * count,
        scratch_shapes=[
            pltpu.VMEM((n, d), f32),
            pltpu.VMEM((2, d, wide), bf),
            pltpu.VMEM((2, wide, d), bf),
            pltpu.SemaphoreType.DMA((2, 2)),
        ],
        input_output_aliases={base + i: i for i in range(carried)},
        cost_estimate=pl.CostEstimate(
            flops=6 * n * d * wide * pieces,
            bytes_accessed=4 * (n + d) * wide * pieces + 6 * n * d,
            transcendentals=2 * n * wide * pieces,
        ),
        compiler_params=params(),
    )(order, *blocks, grads, *w_in, *w_out, *(kept or ()))
    return out[:4], out[4:]


def row_chunk(n):
    for parts in (2, 3, 4):
        if n > 320 and n % parts == 0 and (n // parts) % 16 == 0:
            return n // parts
    return n


def expert_result(order, act, grad_pre, rows, w_out, blocks):
    n, d = rows.shape
    wide = w_out[0].shape[0]
    pieces = len(w_out)
    half = pieces // 2
    each = n // blocks
    chunk = row_chunk(n)

    def expert_outputs(order_ref, act_ref, gp_ref, rows_ref, *refs):
        w = refs[:pieces]
        near_ref, far_ref, out_ref, total, buf, sem = refs[pieces:]
        p = pl.program_id(0)
        slot = lax.rem(p, 2)
        stream(pieces, lambda i: (pltpu.make_async_copy(w[i], buf.at[i % 2], sem.at[i % 2]),))
        for r in range(n // chunk):
            at = slice(r * chunk, (r + 1) * chunk)
            part = dot_nn(act_ref[at], buf[slot])

            @pl.when(p == 0)
            def _(at=at, part=part):
                total[at] = part

            @pl.when(p > 0)
            def _(at=at, part=part):
                total[at] += part

        term = dot_tn(rows_ref[...], gp_ref[...]).astype(bf)

        @pl.when(p < half)
        def _():
            near_ref[0] = term

        @pl.when(p >= half)
        def _():
            far_ref[0] = term

        @pl.when(p == pieces - 1)
        def _():
            for k in range(blocks):
                out_ref[order_ref[k]] = total[k * each : (k + 1) * each].astype(bf)

    tile = pl.BlockSpec((n, wide), lambda p: (0, p))
    return pl.pallas_call(
        expert_outputs,
        grid=(pieces,),
        in_specs=[pl.BlockSpec(memory_space=pltpu.SMEM), tile, tile, pl.BlockSpec((n, d), lambda p: (0, 0))]
        + [pl.BlockSpec(memory_space=pl.ANY)] * pieces,
        out_specs=[
            pl.BlockSpec((1, d, wide), lambda p: (jnp.minimum(p, half - 1), 0, 0)),
            pl.BlockSpec((1, d, wide), lambda p: (jnp.maximum(p - half, 0), 0, 0)),
            pl.BlockSpec((blocks, each, d), lambda p: (0, 0, 0)),
        ],
        out_shape=[jax.ShapeDtypeStruct((half, d, wide), bf)] * 2 + [jax.ShapeDtypeStruct((blocks, each, d), bf)],
        scratch_shapes=[
            pltpu.VMEM((n, d), f32),
            pltpu.VMEM((2, wide, d), bf),
            pltpu.SemaphoreType.DMA((2,)),
        ],
        cost_estimate=pl.CostEstimate(
            flops=4 * n * d * wide * pieces,
            bytes_accessed=4 * (n + d) * wide * pieces + 2 * n * d,
            transcendentals=0,
        ),
        compiler_params=params(),
    )(order, act, grad_pre, rows, *w_out)


def expert_weights(left, right, pieces):
    half = pieces // 2
    n, d = right.shape
    wide = left.shape[1] // pieces

    def expert_weight_grads(left_ref, right_ref, near_ref, far_ref):
        total = dot_tn(left_ref[...], right_ref[...]).astype(bf)
        p = pl.program_id(0)

        @pl.when(p < half)
        def _():
            near_ref[0] = total

        @pl.when(p >= half)
        def _():
            far_ref[0] = total

    return pl.pallas_call(
        expert_weight_grads,
        grid=(pieces,),
        in_specs=[pl.BlockSpec((n, wide), lambda p: (0, p)), pl.BlockSpec((n, d), lambda p: (0, 0))],
        out_specs=[
            pl.BlockSpec((1, wide, d), lambda p: (jnp.minimum(p, half - 1), 0, 0)),
            pl.BlockSpec((1, wide, d), lambda p: (jnp.maximum(p - half, 0), 0, 0)),
        ],
        out_shape=[jax.ShapeDtypeStruct((half, wide, d), bf)] * 2,
        cost_estimate=pl.CostEstimate(
            flops=2 * n * d * wide * pieces,
            bytes_accessed=2 * (n + d) * wide * pieces + 2 * n * d,
            transcendentals=0,
        ),
        compiler_params=params(),
    )(left, right)


def picks(rows, columns, target, axis):
    at = lax.broadcasted_iota(jnp.int32, (rows, columns), axis)
    return (at == target).astype(f32).astype(bf)


def place(target, x_ref, outs):
    each = outs[0].shape[0]
    group = max(1, min(len(outs), 576 // each))
    for h in range(0, len(outs), group):
        pick = picks(group * each, x_ref.shape[0], target - h * each, 0)
        got = dot_nn(pick, x_ref[...]).astype(bf)
        for k in range(group):
            outs[h + k][...] = got[k * each : (k + 1) * each]


def fetch(target, y_ref):
    return dot_nn(picks(target.shape[0], y_ref.shape[0], target, 1), y_ref[...])


def place_rows(target_row, x, slots):
    n, d = x.shape

    def rows_to_slots(target_ref, x_ref, out_ref):
        place(target_ref[...], x_ref, [out_ref])

    return pl.pallas_call(
        rows_to_slots,
        out_shape=jax.ShapeDtypeStruct((slots, d), bf),
        cost_estimate=pl.CostEstimate(
            flops=2 * n * d * slots, bytes_accessed=2 * (n + slots) * d, transcendentals=0
        ),
        compiler_params=params(),
    )(target_row, x)


def each_chunk(n, body):
    step = 256 if n % 256 == 0 else n

    @pl.loop(0, n // step)
    def _(i):
        body(pl.ds(pl.multiple_of(i * step, step), step))


def add_rows(target_col, returned, hidden):
    n, d = hidden.shape

    def block_outputs(target_ref, y_ref, hid_ref, out_ref):
        def body(at):
            out_ref[at] = (hid_ref[at] + fetch(target_ref[at], y_ref)).astype(bf)

        each_chunk(n, body)

    return pl.pallas_call(
        block_outputs,
        out_shape=jax.ShapeDtypeStruct((n, d), bf),
        cost_estimate=pl.CostEstimate(
            flops=2 * n * d * returned.shape[0], bytes_accessed=10 * n * d, transcendentals=0
        ),
        compiler_params=params(),
    )(target_col, returned, hidden)


def centred_rows(values):
    centre = jnp.mean(values, axis=-1, keepdims=True)
    centred = values - centre
    spread = jnp.mean(centred * centred, axis=-1, keepdims=True)
    return centred, lax.rsqrt(spread + eps)


def norm_grad(values, gain, grad):
    centred, inverse = centred_rows(values)
    unit = centred * inverse
    g = gain * grad
    back = (g - jnp.mean(g, axis=-1, keepdims=True) - unit * jnp.mean(g * unit, axis=-1, keepdims=True)) * inverse
    return back, jnp.sum(grad * unit, axis=0, keepdims=True), jnp.sum(grad, axis=0, keepdims=True)


def projections(place_a, place_b, arrays_a, arrays_b, tokens, rows_in, rows_out, near):
    n, d = tokens.shape
    count = place_a.shape[0]
    rest = rows_in - near
    sources = len(arrays_a)
    per = count // sources

    def norm_and_projections(at_a, at_b, tok_ref, *refs):
        a_refs = refs[:sources]
        b_refs = refs[sources : 2 * sources]
        in_ref, out_ref, norm_ref, normed_ref, q_ref, k_ref, v_ref, norm_buf, sem = refs[2 * sources :]
        norm_copies = []
        copies = []
        for s in range(count):
            a, b = a_refs[s // per], b_refs[s // per]
            norm_copies.append(
                pltpu.make_async_copy(b.at[s % per, pl.ds(rest + rows_out, 8)], norm_buf.at[s], sem.at[3, s])
            )
            to_a = pl.multiple_of(at_a[s] * rows_in, 8)
            to_b = pl.multiple_of(at_b[s] * rows_in + near, 8)
            to_out = pl.multiple_of(at_b[s] * rows_out, 8)
            copies.append(
                pltpu.make_async_copy(a.at[s % per], in_ref.at[pl.ds(to_a, near)], sem.at[0, s])
            )
            copies.append(
                pltpu.make_async_copy(b.at[s % per, pl.ds(0, rest)], in_ref.at[pl.ds(to_b, rest)], sem.at[1, s])
            )
            copies.append(
                pltpu.make_async_copy(
                    b.at[s % per, pl.ds(rest, rows_out)], out_ref.at[pl.ds(to_out, rows_out)], sem.at[2, s]
                )
            )
        for copy in norm_copies + copies:
            copy.start()
        for copy in norm_copies:
            copy.wait()
        norm_ref[...] = jnp.sum(norm_buf[...].astype(f32), axis=0)

        def norm(at):
            centred, inverse = centred_rows(tok_ref[at].astype(f32))
            normed_ref[at] = (centred * inverse * norm_ref[0:1] + norm_ref[2:3]).astype(bf)

        each_chunk(n, norm)
        for copy in copies:
            copy.wait()

        def project(at):
            x = normed_ref[at]
            for i, ref in enumerate((q_ref, k_ref, v_ref)):
                ref[at] = dot_nn(x, in_ref[i * d : (i + 1) * d]).astype(bf)

        each_chunk(n, project)

    vm = pl.BlockSpec(memory_space=pltpu.VMEM)
    sm = pl.BlockSpec(memory_space=pltpu.SMEM)
    raw = pl.BlockSpec(memory_space=pl.ANY)
    return pl.pallas_call(
        norm_and_projections,
        in_specs=[sm, sm, vm] + [raw] * (2 * sources),
        out_specs=[vm] * 7,
        out_shape=[
            jax.ShapeDtypeStruct((count * rows_in, d), bf),
            jax.ShapeDtypeStruct((count * rows_out, d), bf),
            jax.ShapeDtypeStruct((8, d), f32),
        ]
        + [jax.ShapeDtypeStruct((n, d), bf)] * 4,
        scratch_shapes=[pltpu.VMEM((count, 8, d), bf), pltpu.SemaphoreType.DMA((4, count))],
        cost_estimate=pl.CostEstimate(
            flops=6 * n * d * d, bytes_accessed=4 * count * (rows_in + rows_out) * d + 10 * n * d, transcendentals=n
        ),
        compiler_params=params(),
    )(place_a, place_b, tokens, *arrays_a, *arrays_b)


def mix_and_place(target_row, tokens, mixed, all_out, norms, slots, parts):
    n, d = tokens.shape

    def mix_and_norm(target_ref, tok_ref, mixed_ref, w_ref, norm_ref, hid_ref, *refs):
        rows = refs[parts]

        def body(at):
            hidden = tok_ref[at].astype(f32) + dot_nn(mixed_ref[at], w_ref[...])
            hid_ref[at] = hidden
            centred, inverse = centred_rows(hidden)
            rows[at] = (centred * inverse * norm_ref[1:2] + norm_ref[3:4]).astype(bf)

        each_chunk(n, body)
        place(target_ref[...], rows, refs[:parts])

    return pl.pallas_call(
        mix_and_norm,
        out_shape=[jax.ShapeDtypeStruct((n, d), f32)]
        + [jax.ShapeDtypeStruct((slots // parts, d), bf)] * parts,
        scratch_shapes=[pltpu.VMEM((n, d), bf)],
        cost_estimate=pl.CostEstimate(
            flops=2 * n * d * (d + slots), bytes_accessed=8 * n * d + 2 * slots * d + 2 * d * d, transcendentals=n
        ),
        compiler_params=params(),
    )(target_row, tokens, mixed, all_out, norms)


def split_groups(core_ref, total, away_ref, own_ref):
    columns, rows = away_ref.shape[0], away_ref.shape[1]
    core = core_ref[0]
    for y in range(columns):
        away = pl.multiple_of((2 * y + 1 - core) * rows, 8)
        own = pl.multiple_of((2 * y + core) * rows, 8)
        away_ref[y] = total[pl.ds(away, rows)].astype(bf)
        own_ref[y] = total[pl.ds(own, rows)].astype(bf)


def norm_back(core, target_col, backs, hidden, cotangent, mixed, all_out, norms, columns):
    n, d = hidden.shape
    parts = len(backs)
    each = backs[0].shape[0]
    rows = d // (2 * columns)

    def second_norm_back(core_ref, target_ref, *refs):
        back_refs = refs[:parts]
        hid_ref, cot_ref, mixed_ref, w_ref, norm_ref = refs[parts : parts + 5]
        gh_ref, gm_ref, sum_ref, away_ref, own_ref, low, total, slots = refs[parts + 5 :]
        sum_ref[...] = jnp.zeros_like(sum_ref)
        for k in range(parts):
            slots[k * each : (k + 1) * each] = back_refs[k][...]

        def body(at):
            grad = fetch(target_ref[at], slots)
            back, gain, bias = norm_grad(hid_ref[at], norm_ref[1:2], grad)
            grad_hidden = cot_ref[at].astype(f32) + back
            gh_ref[at] = grad_hidden
            sum_ref[0:1] += gain
            sum_ref[1:2] += bias
            low[at] = grad_hidden.astype(bf)
            gm_ref[at] = dot_nt(low[at], w_ref[...]).astype(bf)

        each_chunk(n, body)
        total[...] = dot_tn(mixed_ref[...], low[...])
        split_groups(core_ref, total, away_ref, own_ref)

    sm = pl.BlockSpec(memory_space=pltpu.SMEM)
    vm = pl.BlockSpec(memory_space=pltpu.VMEM)
    return pl.pallas_call(
        second_norm_back,
        in_specs=[sm] + [vm] * (6 + parts),
        out_specs=[vm] * 5,
        out_shape=[
            jax.ShapeDtypeStruct((n, d), f32),
            jax.ShapeDtypeStruct((n, d), bf),
            jax.ShapeDtypeStruct((8, d), f32),
            jax.ShapeDtypeStruct((columns, rows, d), bf),
            jax.ShapeDtypeStruct((columns, rows, d), bf),
        ],
        scratch_shapes=[pltpu.VMEM((n, d), bf), pltpu.VMEM((d, d), f32), pltpu.VMEM((each * parts, d), bf)],
        cost_estimate=pl.CostEstimate(
            flops=6 * n * d * d, bytes_accessed=16 * n * d + 4 * d * d, transcendentals=n
        ),
        compiler_params=params(),
    )(core, target_col, *backs, hidden, cotangent, mixed, all_out, norms)


def projection_grads(core, normed, grads, columns):
    n, d = normed.shape
    rows = 3 * d // (2 * columns)

    def projection_weight_grads(core_ref, x_ref, *refs):
        away_ref, own_ref, total = refs[3:]
        for i in range(3):
            total[i * d : (i + 1) * d] = dot_tn(x_ref[...], refs[i][...])
        split_groups(core_ref, total, away_ref, own_ref)

    sm = pl.BlockSpec(memory_space=pltpu.SMEM)
    vm = pl.BlockSpec(memory_space=pltpu.VMEM)
    return pl.pallas_call(
        projection_weight_grads,
        in_specs=[sm] + [vm] * 4,
        out_specs=[vm] * 2,
        out_shape=[jax.ShapeDtypeStruct((columns, rows, grads[0].shape[1]), bf)] * 2,
        scratch_shapes=[pltpu.VMEM((3 * d, grads[0].shape[1]), f32)],
        cost_estimate=pl.CostEstimate(
            flops=6 * n * d * d, bytes_accessed=8 * n * d + 6 * d * d, transcendentals=0
        ),
        compiler_params=params(),
    )(core, normed, *grads)


def first_norm_back(grads, all_in, tokens, norms, grad_hidden, sums_second):
    n, d = tokens.shape

    def input_grads(q_ref, k_ref, v_ref, w_ref, tok_ref, norm_ref, gh_ref, second_ref, out_ref, sum_ref):
        sum_ref[...] = jnp.zeros_like(sum_ref)
        sum_ref[1:2] = second_ref[0:1]
        sum_ref[3:4] = second_ref[1:2]

        def body(at):
            grad = dot_nt(q_ref[at], w_ref[0:d])
            grad += dot_nt(k_ref[at], w_ref[d : 2 * d])
            grad += dot_nt(v_ref[at], w_ref[2 * d :])
            back, gain, bias = norm_grad(tok_ref[at].astype(f32), norm_ref[0:1], grad)
            out_ref[at] = gh_ref[at] + back
            sum_ref[0:1] += gain
            sum_ref[2:3] += bias

        each_chunk(n, body)

    return pl.pallas_call(
        input_grads,
        out_shape=[jax.ShapeDtypeStruct((n, d), f32), jax.ShapeDtypeStruct((4, d), f32)],
        cost_estimate=pl.CostEstimate(
            flops=6 * n * d * d, bytes_accessed=16 * n * d + 6 * d * d, transcendentals=n
        ),
        compiler_params=params(),
    )(*grads, all_in, tokens, norms, grad_hidden, sums_second)


def from_others(x, axis):
    n = lax.axis_size(axis)
    return [x] + [lax.ppermute(x, axis, [(i, (i - s) % n) for i in range(n)]) for s in range(1, n)]


def gather_stage(x, axis):
    return jnp.stack(from_others(x, axis))


def block_places(order, sizes):
    place = jnp.arange(math.prod(sizes.values()), dtype=jnp.int32)
    where = {}
    step = 1
    for axis in order:
        where[axis] = (place // step + lax.axis_index(axis)) % sizes[axis]
        step *= sizes[axis]
    whole = 0
    for axis in EVERY:
        whole = whole * sizes[axis] + where[axis]
    return whole.astype(jnp.int32)


def gather_parameters(attn_in, attn_out, ln_gain, ln_bias, tokens, during):
    rows_in, d = attn_in.shape
    rows_out = attn_out.shape[0]
    span = ln_gain.shape[1]
    sizes = {axis: lax.axis_size(axis) for axis in EVERY}
    count = math.prod(sizes.values())
    me = lax.axis_index(EVERY)
    own = jnp.concatenate([ln_gain, ln_bias], axis=0)
    norm = jnp.where(lane_iota((4, d)) // span == me, jnp.tile(own, (1, count)), 0)
    norm = jnp.pad(norm, ((0, 4), (0, 0)))
    if rows_in % 8 or rows_out % 8:
        whole_in, whole_out = [lax.all_gather(a, EVERY, axis=0, tiled=True) for a in (attn_in, attn_out)]
        whole_norm = lax.all_gather(norm, EVERY, axis=0, tiled=False)
        at = jnp.arange(1, dtype=jnp.int32)
        near = 3 * d // 16 * 8
        second = jnp.concatenate([whole_in[near:], whole_out, jnp.sum(whole_norm.astype(f32), axis=0).astype(bf)])
        return projections(at, at, [whole_in[None, :near]], [second[None]], tokens, 3 * d, d, near), during
    near = 56 if rows_in == 72 else rows_in // 16 * 8
    b = jnp.concatenate([attn_in[near:], attn_out, norm], axis=0)
    order_a = ("z", "x", "y", "core")
    order_b = ("y", "z", "x", "core")
    a = gather_stage(attn_in[:near], "z")
    a, during = lax.optimization_barrier((a, during))
    b = gather_stage(b, "y")
    a = gather_stage(a, "x")
    b = gather_stage(b, "z")
    a = gather_stage(a, "y")
    b = gather_stage(b, "x")
    a = a.reshape(count // 2, near, d)
    b = b.reshape(count // 2, -1, d)
    out = projections(
        block_places(order_a, sizes),
        block_places(order_b, sizes),
        from_others(a, "core"),
        from_others(b, "core"),
        tokens,
        rows_in,
        rows_out,
        near,
    )
    return out, during


def other_core(x):
    return lax.ppermute(x, "core", [(0, 1), (1, 0)])


def scatter_pieces(near, far):
    columns = near.shape[0]
    other = other_core(far)
    terms = [near[0], other[0]]
    for s in range(1, columns):
        pair = (near[s].astype(f32) + other[s].astype(f32)).astype(bf)
        terms.append(lax.ppermute(pair, "y", [(i, (i + s) % columns) for i in range(columns)]))
    return terms


def scatter_rows(away, own, shared=None):
    columns, rows, d = own.shape
    ring = lax.axis_size("z") * lax.axis_size("x")
    pair = (own.astype(f32) + other_core(away).astype(f32)).astype(bf).reshape(columns * ring, rows // ring, d)
    if shared is not None:
        pair = jnp.concatenate([pair, jnp.broadcast_to(shared[None], (columns * ring,) + shared.shape)], axis=1)
    return lax.all_to_all(pair, RING, split_axis=0, concat_axis=0, tiled=True)


def core_sums(terms):
    pair = terms + other_core(terms)
    high = pair.astype(bf)
    return jnp.concatenate([high, (pair - high.astype(f32)).astype(bf)], axis=0)


def swap(x):
    return lax.all_to_all(x, EXPERT, split_axis=0, concat_axis=0, tiled=True)


def trade(x, step):
    if step == 0:
        return x
    experts = lax.axis_size("z") * lax.axis_size("x")
    return lax.ppermute(x, EXPERT, [(i, i ^ step) for i in range(experts)])


def after(x, *others):
    return lax.optimization_barrier((x, others))[0]


def summed(terms):
    return sum(term.astype(f32) for term in terms)


def shards(tokens, lengths, routes, attn_in, attn_out, ln_gain, ln_bias, w_in, w_out, cotangent):
    row_count, d = tokens.shape
    limit = lengths[0]
    columns = lax.axis_size("y")
    experts = lax.axis_size("z") * lax.axis_size("x")
    capacity = max(2, 9 * row_count // (8 * experts))
    slot_total = experts * capacity
    core = lax.axis_index("core").astype(jnp.int32)[None]
    me = lax.axis_index(EXPERT).astype(jnp.int32)
    paired = experts == 8 and capacity % 16 == 0

    valid = jnp.arange(row_count) < limit
    onehot = ((routes[:, None] == jnp.arange(experts)[None, :]) & valid[:, None]).astype(jnp.int32)
    ranks = jnp.sum((jnp.cumsum(onehot, axis=0) - 1) * onehot, axis=1)
    target = jnp.where(valid, routes * capacity + ranks, 2 * slot_total)
    if paired:
        near_target = jnp.where(valid, (routes ^ me) * capacity + ranks, 2 * slot_total)
        blocks, each = experts, capacity
        order = jnp.arange(experts, dtype=jnp.int32) ^ me
        groups = [(0, 4), (4, 2), (6, 2)]
    else:
        near_target = target
        blocks, each = 1, slot_total
        order = jnp.zeros((1,), jnp.int32)
        groups = [(0, 1)]

    placed = place_rows(target[None, :], cotangent, slot_total)
    gathered, placed = gather_parameters(attn_in, attn_out, ln_gain, ln_bias, tokens, placed)
    all_in, all_out, norms, normed, query, key_rows, value_rows = gathered
    grads = swap(placed.reshape(experts, capacity, d)).reshape(blocks, each, d)
    in_near = from_others(w_in[0], "y")
    out_near = from_others(w_out[0], "y")

    tile = min(256, row_count)
    mixed, query_wide, key_wide = attn_fwd(lengths, query, key_rows, value_rows, tile)
    mixed, in_near = lax.optimization_barrier((mixed, in_near))
    hidden, *sends = mix_and_place(near_target[None, :], tokens, mixed, all_out, norms, slot_total, blocks)
    if paired:
        rows = [trade(x, k) for k, x in enumerate(sends)]
    else:
        rows = [swap(sends[0].reshape(experts, capacity, d)).reshape(each, d)]
    in_pieces = in_near + [other_core(x) for x in in_near]
    out_pieces = out_near + [other_core(x) for x in out_near]

    kept, backs = None, []
    for number, (first, count) in enumerate(groups):
        taken = rows[first : first + count]
        if number == 2:
            taken, backs[:4] = lax.optimization_barrier((taken, backs[:4]))
        kept, outs = expert_group(order, first, taken, grads, in_pieces, out_pieces, kept, slot_total)
        if paired:
            backs = backs + [trade(x, first + k) for k, x in enumerate(outs)]
        else:
            backs = [swap(outs[0].reshape(experts, capacity, d)).reshape(each, d)]
    act, grad_pre, all_rows, all_grads = kept
    act, backs[:6] = lax.optimization_barrier((act, backs[:6]))
    *in_terms, result = expert_result(order, act, grad_pre, all_rows, out_pieces, blocks)
    returned = swap(result.reshape(experts, capacity, d)).reshape(-1, d)

    grad_hidden, grad_mixed, sums_second, away, own = norm_back(
        core, near_target[:, None], after(backs, result), hidden, cotangent, mixed, all_out, norms, columns
    )
    attn_out_terms = scatter_rows(away, own)
    in_terms = scatter_pieces(*after(in_terms, grad_mixed))
    out_terms = expert_weights(after(act, grad_mixed), all_grads, len(in_pieces))
    grads_qkv = attn_bwd(query_wide, key_wide, value_rows, mixed, after(grad_mixed, out_terms), tile)
    out_terms = scatter_pieces(*out_terms)
    away, own = projection_grads(core, normed, after(grads_qkv, in_terms), columns)
    grad_tokens, norm_sums = first_norm_back(
        after(grads_qkv, away), all_in, tokens, norms, after(grad_hidden, attn_out_terms), sums_second
    )
    attn_in_terms = scatter_rows(away, own, core_sums(norm_sums))
    block_out = add_rows(target[:, None], after(returned, norm_sums), hidden)
    sums = jnp.sum(attn_in_terms.astype(f32), axis=0)
    rows_in = attn_in.shape[0]
    span = ln_gain.shape[1]
    sums_norm = lax.dynamic_slice_in_dim(
        sums[rows_in : rows_in + 4] + sums[rows_in + 4 :], lax.axis_index(EVERY) * span, span, axis=1
    )
    return (
        block_out,
        grad_tokens,
        sums[:rows_in],
        jnp.sum(attn_out_terms.astype(f32), axis=0),
        sums_norm[:2],
        sums_norm[2],
        sums_norm[3],
        summed(in_terms)[None],
        summed(out_terms)[None],
    )


def solution(mesh):
    columns, experts = mesh.devices.shape
    across = 1
    while (2 * across) ** 2 <= experts:
        across *= 2
    fine = Mesh(mesh.devices.reshape(columns // 2, 2, experts // across, across), EVERY)
    every = P(EVERY)
    dp = ("y", "core")
    in_specs = (
        P(EVERY, None),
        every,
        every,
        P(EVERY, None),
        P(EVERY, None),
        P(None, EVERY),
        P(None, EVERY),
        P(EXPERT, None, dp),
        P(EXPERT, dp, None),
        P(EVERY, None),
    )
    out_specs = (
        P(EVERY, None),
        P(EVERY, None),
        P(EVERY, None),
        P(EVERY, None),
        P(None, EVERY),
        every,
        every,
        P(EXPERT, None, dp),
        P(EXPERT, dp, None),
    )
    return jax.shard_map(shards, mesh=fine, in_specs=in_specs, out_specs=out_specs, check_vma=False)
```
